32 devices in a mesh: seq: 8 (over y, x, core), tp: 4 (over z).
Axes of the slice: x: 2, y: 2, z: 4, core: 2. Of those that a mesh axis runs over, the one named last changes fastest.
Arguments:
- features: bfloat16 [576, 5376], P('seq', 'tp'), may hold values from -6 to 6
- gate_logits: float32 [1, 3], replicated, may hold values from -3 to 3
- proj_weight: bfloat16 [5376, 8192], P('tp'), may hold values from -0.125 to 0.125
- positions: int32 [576], replicated, may hold values from 0 to 12287, as said below
- text: bfloat16 [12288, 8192], P(('seq', 'tp')), may hold values from -6 to 6
Outputs:
- mixed: bfloat16 [12288, 8192], P(('seq', 'tp'))
The draws below stay inside these ranges and needn't reach their ends.
Inputs may be any that keep to these rules, and one draw needn't show every extreme that they name: All positions are distinct. Of the 72 image tokens of one index of seq (rows of an aligned block), at most 9 fall into one aligned block of 1536 positions, and exactly 9 do for some pair of blocks. At most 18 image tokens in all fall into one aligned block of 384 positions, and exactly 18 do in the first such block of every aligned block of 1536 positions.
All inputs are finite; a program needn't handle non-finite values.
Results may differ from the reference program's by a relative error of at most 0.005.
Values may be sent and summed in bfloat16 or wider, within the bound.
A program may use at most 64 MiB of HBM per device.

```python
import jax
import jax.numpy as jnp

D = 8192
CLIP_C = 1024
CNX_C = 3072
C = 5376
SIDE = 24
IMG_DEV = 72
TOK_DEV = 1536
TOKENS = 12288
IMG_TOK = 576
IMAGES = 1
N_SEQ = 8
N_TP = 4


def draw_positions(key, part):
    key_hot, key_order, key_place = jax.random.split(jax.random.fold_in(key, 7), 3)
    capacity = (IMG_DEV + N_SEQ - 1) // N_SEQ
    sub_capacity = (N_SEQ * capacity + N_TP - 1) // N_TP
    sub_rows = TOK_DEV // N_TP
    hot_flags = (jax.random.randint(key_hot, (N_SEQ,), 0, 8) == 0).astype(jnp.int32)
    raw_scores = jax.random.randint(key_order, (N_SEQ, capacity, N_SEQ), 0, N_SEQ)
    scores = raw_scores * N_SEQ + jnp.arange(N_SEQ, dtype=jnp.int32)[None, None, :]
    last_round = (jnp.arange(capacity, dtype=jnp.int32) == capacity - 1).astype(jnp.int32)
    scores = scores - last_round[None, :, None] * hot_flags[None, None, :] * (N_SEQ * N_SEQ)
    targets = jnp.argsort(scores, axis=2).astype(jnp.int32)
    targets = targets.reshape(N_SEQ, capacity * N_SEQ)[:, :IMG_DEV].reshape(N_SEQ * IMG_DEV)
    row_order = jnp.argsort(targets, stable=True).astype(jnp.int32)
    sorted_targets = targets[row_order]
    group_first = jnp.searchsorted(sorted_targets, sorted_targets, side='left').astype(jnp.int32)
    rank_sorted = jnp.arange(N_SEQ * IMG_DEV, dtype=jnp.int32) - group_first
    ranks = jnp.zeros((N_SEQ * IMG_DEV,), jnp.int32).at[row_order].set(rank_sorted)
    sub_block = ranks // sub_capacity
    sub_rank = ranks % sub_capacity
    place_scores = jax.random.randint(key_place, (N_SEQ, N_TP, sub_rows), 0, sub_rows) * sub_rows
    place_scores = place_scores + jnp.arange(sub_rows, dtype=jnp.int32)[None, None, :]
    placement_table = jnp.argsort(place_scores, axis=2).astype(jnp.int32)
    offsets = sub_block * sub_rows + placement_table[targets, sub_block, sub_rank]
    return (targets * TOK_DEV + offsets).astype(jnp.int32)


def levels(stream_key, dims, cuts, least, high):
    level, own = 1.0, jax.random.fold_in(stream_key, 6)
    for axis_at, blocks in cuts:
        draws = jnp.exp(jax.random.uniform(jax.random.fold_in(own, axis_at), (blocks,), jnp.float32, least / len(cuts), high / len(cuts)))
        level = level * jnp.repeat(draws, dims[axis_at] // blocks).reshape([-1 if axis == axis_at else 1 for axis in range(len(dims))])
    return level


def normal_values(stream_key, shape, deviation, reach, pieces=(), kind=jnp.bfloat16):
    gain = levels(stream_key, shape, pieces, -0.22, 0.18) if pieces else 1.0
    result = jax.random.normal(stream_key, shape, jnp.float32) * deviation * gain
    return jnp.minimum(jnp.maximum(result, -reach), reach).astype(kind)


def setup_inputs(seed: int = 0) -> dict:
    key_of = jax.random.split(jax.random.key(seed), 6)
    return {
        "features": normal_values(key_of[0], (IMG_TOK, C), 1.0, 6.0, ((0, 8), (1, 4))),
        "gate_logits": jnp.clip(jax.random.uniform(key_of[1], (IMAGES, 3), jnp.float32, -3.0, 3.0), -3.0, 3.0),
        "proj_weight": normal_values(key_of[2], (C, D), (C // 3) ** -0.5, 0.125, ((0, 4),)),
        "positions": draw_positions(jax.random.fold_in(key_of[5], 71), 0),
        "text": normal_values(key_of[4], (TOKENS, D), 1.0, 6.0, ((0, 32),)),
    }


def reference(features, gate_logits, proj_weight, positions, text):
    total_rows = features.shape[0]
    image_ids = jnp.arange(total_rows, dtype=jnp.int32) // (SIDE * SIDE)
    row_gates = jax.nn.sigmoid(gate_logits[image_ids].astype(jnp.float32))
    channel = jnp.arange(C, dtype=jnp.int32)
    encoder = (channel >= CLIP_C).astype(jnp.int32) + (channel >= CLIP_C + CNX_C).astype(jnp.int32)
    gates = row_gates[:, encoder]
    gated = (features.astype(jnp.float32) * gates).astype(jnp.bfloat16)
    slice_width = C // N_TP
    summed = jnp.zeros((total_rows, D), jnp.float32)
    for column in range(N_TP):
        lower = column * slice_width
        partial_value = jnp.dot(gated[:, lower:lower + slice_width], proj_weight[lower:lower + slice_width],
                          preferred_element_type=jnp.float32).astype(jnp.bfloat16)
        summed = summed + partial_value.astype(jnp.float32)
    embedded = summed.astype(jnp.bfloat16)
    return text.at[positions].set(embedded)
```

```python
import functools

import jax
import jax.numpy as jnp
from jax import lax
from jax.experimental import pallas as pl
from jax.experimental.pallas import tpu as pltpu
from jax.sharding import PartitionSpec as P

CLIP_C = 1024
CNX_C = 3072
SIDE = 24
MESH = pl.DeviceIdType.MESH
CHUNK = 512


def up(value, unit):
    return -(-value // unit) * unit


def iota(shape, dim):
    return lax.broadcasted_iota(jnp.int32, shape, dim)


def floor_div(value, unit):
    return ((value.astype(jnp.float32) + 0.5) * (1.0 / unit)).astype(jnp.int32)


def to_row(column):
    size = column.shape[0]
    eye = iota((size, size), 0) == iota((size, size), 1)
    return jnp.sum(jnp.where(eye, column, 0), axis=0, keepdims=True)


def to_column(row):
    size = row.shape[1]
    eye = iota((size, size), 0) == iota((size, size), 1)
    return jnp.sum(jnp.where(eye, row, 0), axis=1, keepdims=True)


class Plan:
    def __init__(self, n_seq, n_tp, rows, width, depth, rows_here):
        self.n_seq, self.n_tp, self.rows, self.width = n_seq, n_tp, rows, width
        self.depth, self.rows_here = depth, rows_here
        self.cap = -(-rows // n_seq)
        self.cap_pad = up(self.cap, 16)
        self.slots = n_seq * self.cap_pad
        self.sub_cap = -(-(n_seq * self.cap) // n_tp)
        self.packed = up(n_tp * self.sub_cap, 8)
        self.groups = self.packed // 8
        self.chunks = depth // CHUNK
        self.first = [self.sub_cap * t // 8 for t in range(n_tp)]
        self.last = [-(-self.sub_cap * (t + 1) // 8) for t in range(n_tp)]
        self.window = max(b - a for a, b in zip(self.first, self.last))

    def right(self, t):
        return self.first[t + 1], self.groups

    def left(self, t):
        return 0, self.last[t - 1]


def join_kernel(
    plan, pos_ref, logit_ref, feat_ref, w_ref,
    out_ref, row_ref,
    wbuf, outgoing, arrived, picked, part, send_r, send_l, recv_r, recv_l,
    w_sem, x_send, x_recv, rs_send, rs_recv, ls_send, ls_recv,
):
    n_seq, n_tp, rows = plan.n_seq, plan.n_tp, plan.rows
    s = lax.axis_index("seq")
    t = lax.axis_index("tp")

    barrier = pltpu.get_barrier_semaphore()
    for step in range(1, n_seq):
        pl.semaphore_signal(barrier, inc=1, device_id={"seq": lax.rem(s + step, n_seq)}, device_id_type=MESH)

    @pl.when(t > 0)
    def _():
        pl.semaphore_signal(barrier, inc=1, device_id={"tp": t - 1}, device_id_type=MESH)

    @pl.when(t < n_tp - 1)
    def _():
        pl.semaphore_signal(barrier, inc=1, device_id={"tp": t + 1}, device_id_type=MESH)

    def weight_copy(k):
        return pltpu.make_async_copy(
            w_ref.at[:, pl.ds(pl.multiple_of(k * CHUNK, CHUNK), CHUNK)], wbuf.at[k], w_sem.at[k]
        )

    @pl.loop(0, plan.chunks)
    def _(k):
        weight_copy(k).start()

    row_id = s * rows + iota((rows, 1), 0)
    gates = []
    for encoder in range(3):
        picked_logit = jnp.zeros((rows, 1), jnp.float32)
        for image in range(logit_ref.shape[0]):
            here = (row_id >= image * SIDE * SIDE) & (row_id < (image + 1) * SIDE * SIDE)
            picked_logit = jnp.where(here, logit_ref[image, encoder], picked_logit)
        gates.append(jax.nn.sigmoid(picked_logit))
    channel = t * plan.width + iota((rows, plan.width), 1)
    gate = jnp.where(channel < CLIP_C, gates[0], jnp.where(channel < CLIP_C + CNX_C, gates[1], gates[2]))
    gated = (feat_ref[...].astype(jnp.float32) * gate).astype(jnp.bfloat16)

    seq_rows = plan.rows_here * n_tp
    own_pos = pos_ref[pl.ds(s, 1), :]
    own_target = floor_div(own_pos, seq_rows)
    target_col = to_column(own_target)
    before = iota((rows, rows), 0) < iota((rows, rows), 1)
    own_slot = jnp.sum(
        jnp.where((target_col == own_target) & before, 1, 0), axis=0, keepdims=True
    )
    address = own_target * plan.cap_pad + own_slot
    choose = (address == iota((plan.slots, rows), 0)).astype(jnp.float32).astype(jnp.bfloat16)
    outgoing[...] = (
        jnp.dot(choose, gated, preferred_element_type=jnp.float32)
        .astype(jnp.bfloat16)
        .reshape(n_seq, plan.cap_pad, plan.width)
    )

    neighbours = jnp.where(t > 0, 1, 0) + jnp.where(t < n_tp - 1, 1, 0)
    pl.semaphore_wait(barrier, n_seq - 1 + neighbours)

    def exchange(step):
        peer = lax.rem(s + step, n_seq)
        return pltpu.make_async_remote_copy(
            src_ref=outgoing.at[peer],
            dst_ref=arrived.at[s],
            send_sem=x_send.at[step],
            recv_sem=x_recv.at[step],
            device_id={"seq": peer},
            device_id_type=MESH,
        )

    for step in range(1, n_seq):
        exchange(step).start()
    arrived[s] = outgoing[s]

    positions = pos_ref[...]
    offset = positions - s * seq_rows
    here = (offset >= 0) & (offset < seq_rows)
    earlier = before.astype(jnp.float32).astype(jnp.bfloat16)
    count = jnp.dot(
        here.astype(jnp.float32).astype(jnp.bfloat16), earlier, preferred_element_type=jnp.float32
    ).astype(jnp.int32)
    count = jnp.where(here, count, -1)
    slot_shape = (n_seq, plan.cap_pad, rows)
    hit = count.reshape(n_seq, 1, rows) == iota(slot_shape, 1)
    offset_of = jnp.where(hit, offset.reshape(n_seq, 1, rows) + 1, 0).reshape(plan.slots, rows)
    offset_col = jnp.sum(offset_of, axis=1, keepdims=True) - 1
    valid_col = offset_col >= 0
    sub_col = jnp.where(valid_col, floor_div(offset_col, plan.rows_here), -1)
    sub_row = to_row(sub_col)
    offset_row = to_row(offset_col)
    square = (plan.slots, plan.slots)
    rank_row = jnp.sum(
        jnp.where((sub_col == sub_row) & (iota(square, 0) < iota(square, 1)), 1, 0), axis=0, keepdims=True
    )
    packed_row = jnp.where(sub_row >= 0, sub_row * plan.sub_cap + rank_row, -1)
    picking = (
        (packed_row == iota((plan.packed, plan.slots), 0)).astype(jnp.float32).astype(jnp.bfloat16)
    )
    window = plan.window * 8
    base = lax.div(plan.sub_cap * t, 8) * 8
    mine = (packed_row == base + iota((window, plan.slots), 0)) & (sub_row == t)
    local = jnp.sum(
        jnp.where(mine, offset_row - t * plan.rows_here + 1, 0), axis=1, keepdims=True
    ) - 1
    row_ref[...] = jnp.broadcast_to(local, row_ref.shape)

    for step in range(1, n_seq):
        exchange(step).wait_recv()
    picked[...] = jnp.dot(
        picking, arrived[...].reshape(plan.slots, plan.width), preferred_element_type=jnp.float32
    ).astype(jnp.bfloat16)

    def send_right(k, i):
        lo, hi = plan.right(i)
        return pltpu.make_async_remote_copy(
            src_ref=send_r.at[k, pl.ds(lo, hi - lo)],
            dst_ref=recv_r.at[k, pl.ds(lo, hi - lo)],
            send_sem=rs_send.at[k],
            recv_sem=rs_recv.at[k],
            device_id={"tp": lax.rem(t + 1, n_tp)},
            device_id_type=MESH,
        )

    def send_left(k, i):
        lo, hi = plan.left(i)
        return pltpu.make_async_remote_copy(
            src_ref=send_l.at[k, pl.ds(lo, hi - lo)],
            dst_ref=recv_l.at[k, pl.ds(lo, hi - lo)],
            send_sem=ls_send.at[k],
            recv_sem=ls_recv.at[k],
            device_id={"tp": lax.rem(t + n_tp - 1, n_tp)},
            device_id_type=MESH,
        )

    @pl.loop(0, plan.chunks)
    def _(k):
        weight_copy(k).wait()
        result = jnp.dot(picked[...], wbuf[k], preferred_element_type=jnp.float32)
        result = result.reshape(plan.groups, 8, CHUNK)
        part[k] = result

        @pl.when(t == 0)
        def _():
            lo, hi = plan.right(0)
            send_r[k, lo:hi] = result[lo:hi].astype(jnp.bfloat16)
            send_right(k, 0).start()

        @pl.when(t == n_tp - 1)
        def _():
            lo, hi = plan.left(n_tp - 1)
            send_l[k, lo:hi] = result[lo:hi].astype(jnp.bfloat16)
            send_left(k, n_tp - 1).start()

    for i in range(n_tp):

        @pl.when(t == i)
        def _(i=i):
            first, last = plan.first[i], plan.last[i]

            @pl.loop(0, plan.chunks)
            def _(k):
                total = part[k, first:last]
                if i > 0:
                    send_right(k, i - 1).wait_recv()
                    if i < n_tp - 1:
                        lo, hi = plan.right(i)
                        send_r[k, lo:hi] = (
                            part[k, lo:hi] + recv_r[k, lo:hi].astype(jnp.float32)
                        ).astype(jnp.bfloat16)
                        send_right(k, i).start()
                    total = total + recv_r[k, first:last].astype(jnp.float32)
                if i < n_tp - 1:
                    send_left(k, i + 1).wait_recv()
                    if i > 0:
                        lo, hi = plan.left(i)
                        send_l[k, lo:hi] = (
                            part[k, lo:hi] + recv_l[k, lo:hi].astype(jnp.float32)
                        ).astype(jnp.bfloat16)
                        send_left(k, i).start()
                    total = total + recv_l[k, first:last].astype(jnp.float32)
                columns = pl.ds(pl.multiple_of(k * CHUNK, CHUNK), CHUNK)
                out_ref[0 : last - first, :, columns] = total.astype(jnp.bfloat16)
                if last - first < plan.window:
                    out_ref[last - first :, :, columns] = jnp.zeros(
                        (plan.window - (last - first), 8, CHUNK), jnp.bfloat16
                    )

            @pl.loop(0, plan.chunks)
            def _(k):
                if i < n_tp - 1:
                    send_right(k, i).wait_send()
                if i > 0:
                    send_left(k, i).wait_send()

    for step in range(1, n_seq):
        exchange(step).wait_send()


def place_kernel(row_ref, summed_ref, text_ref, out_ref):
    block = text_ref.shape[0]
    window = summed_ref.shape[0] * 8
    local = row_ref[0:1, :] - pl.program_id(0) * block
    hits = (local == iota((block, window), 0)).astype(jnp.float32)
    filled = jnp.sum(hits, axis=1, keepdims=True) > 0.5
    values = summed_ref[...].reshape(window, text_ref.shape[1])
    placed = jnp.dot(hits.astype(jnp.bfloat16), values, preferred_element_type=jnp.float32)
    out_ref[...] = jnp.where(filled, placed.astype(jnp.bfloat16), text_ref[...])


def shards(features, gate_logits, proj_weight, positions, text):
    n_seq, n_tp = lax.axis_size("seq"), lax.axis_size("tp")
    rows, width = features.shape
    depth = proj_weight.shape[1]
    rows_here = text.shape[0]
    plan = Plan(n_seq, n_tp, rows, width, depth, rows_here)
    vmem = pl.BlockSpec(memory_space=pltpu.VMEM)
    moving = pltpu.VMEM((plan.chunks, plan.groups, 8, CHUNK), jnp.bfloat16)
    summed, local_rows = pl.pallas_call(
        functools.partial(join_kernel, plan),
        out_shape=(
            jax.ShapeDtypeStruct((plan.window, 8, depth), jnp.bfloat16),
            jax.ShapeDtypeStruct((plan.window * 8, 128), jnp.int32),
        ),
        in_specs=[
            vmem,
            pl.BlockSpec(memory_space=pltpu.SMEM),
            vmem,
            pl.BlockSpec(memory_space=pl.ANY),
        ],
        out_specs=(vmem, vmem),
        scratch_shapes=[
            pltpu.VMEM((plan.chunks, width, CHUNK), jnp.bfloat16),
            pltpu.VMEM((n_seq, plan.cap_pad, width), jnp.bfloat16),
            pltpu.VMEM((n_seq, plan.cap_pad, width), jnp.bfloat16),
            pltpu.VMEM((plan.packed, width), jnp.bfloat16),
            pltpu.VMEM((plan.chunks, plan.groups, 8, CHUNK), jnp.float32),
            moving, moving, moving, moving,
            pltpu.SemaphoreType.DMA((plan.chunks,)),
            pltpu.SemaphoreType.DMA((n_seq,)),
            pltpu.SemaphoreType.DMA((n_seq,)),
            pltpu.SemaphoreType.DMA((plan.chunks,)),
            pltpu.SemaphoreType.DMA((plan.chunks,)),
            pltpu.SemaphoreType.DMA((plan.chunks,)),
            pltpu.SemaphoreType.DMA((plan.chunks,)),
        ],
        compiler_params=pltpu.CompilerParams(collective_id=0, has_side_effects=True),
        name="join",
    )(positions.reshape(n_seq, rows), gate_logits, features, proj_weight)

    window = plan.window * 8
    local_rows = local_rows[:, 0].reshape(1, window)
    block = 64 if rows_here % 64 == 0 else rows_here
    return pl.pallas_call(
        place_kernel,
        grid=(rows_here // block,),
        out_shape=jax.ShapeDtypeStruct(text.shape, text.dtype),
        in_specs=[
            pl.BlockSpec((1, window), lambda i: (0, 0)),
            pl.BlockSpec((plan.window, 8, depth), lambda i: (0, 0, 0)),
            pl.BlockSpec((block, depth), lambda i: (i, 0)),
        ],
        out_specs=pl.BlockSpec((block, depth), lambda i: (i, 0)),
        compiler_params=pltpu.CompilerParams(vmem_limit_bytes=24 * 1024 * 1024),
        name="place",
    )(local_rows, summed, text)


def solution(mesh):
    return jax.shard_map(
        shards,
        mesh=mesh,
        in_specs=(P("seq", "tp"), P(), P("tp", None), P(), P(("seq", "tp"), None)),
        out_specs=P(("seq", "tp"), None),
        check_vma=False,
    )
```

```python
import functools

import jax
import jax.numpy as jnp
from jax import lax
from jax.experimental import pallas as pl
from jax.experimental.pallas import tpu as pltpu
from jax.sharding import PartitionSpec as P

CLIP_C = 1024
CNX_C = 3072
SIDE = 24
MESH = pl.DeviceIdType.MESH
CHUNK = 512
LAG = 6


def up(value, unit):
    return -(-value // unit) * unit


def iota(shape, dim):
    return lax.broadcasted_iota(jnp.int32, shape, dim)


def floor_div(value, unit):
    return ((value.astype(jnp.float32) + 0.5) * (1.0 / unit)).astype(jnp.int32)


def to_row(column):
    size = column.shape[0]
    eye = iota((size, size), 0) == iota((size, size), 1)
    return jnp.sum(jnp.where(eye, column, 0), axis=0, keepdims=True)


def to_column(row):
    size = row.shape[1]
    eye = iota((size, size), 0) == iota((size, size), 1)
    return jnp.sum(jnp.where(eye, row, 0), axis=1, keepdims=True)


class Plan:
    def __init__(self, n_seq, n_tp, rows, width, depth, rows_here):
        self.n_seq, self.n_tp, self.rows, self.width = n_seq, n_tp, rows, width
        self.depth, self.rows_here = depth, rows_here
        self.cap = -(-rows // n_seq)
        self.cap_pad = up(self.cap, 16)
        self.slots = n_seq * self.cap_pad
        self.sub_cap = -(-(n_seq * self.cap) // n_tp)
        self.packed = up(n_tp * self.sub_cap, 8)
        self.groups = self.packed // 8
        self.chunks = depth // CHUNK
        self.first = [self.sub_cap * t // 8 for t in range(n_tp)]
        self.last = [-(-self.sub_cap * (t + 1) // 8) for t in range(n_tp)]
        self.window = max(b - a for a, b in zip(self.first, self.last))

    def right(self, t):
        return self.first[t + 1], self.groups

    def left(self, t):
        return 0, self.last[t - 1]


def join_kernel(
    plan, flat_ref, logit_ref, feat_ref, w_ref,
    out_ref, row_ref,
    pos_ref, wbuf, outgoing, arrived, picked, part, send_r, send_l, recv_r, recv_l,
    w_sem, x_send, x_recv, rs_send, rs_recv, ls_send, ls_recv,
):
    n_seq, n_tp, rows = plan.n_seq, plan.n_tp, plan.rows
    s = lax.axis_index("seq")
    t = lax.axis_index("tp")

    barrier = pltpu.get_barrier_semaphore()
    for step in range(1, n_seq):
        pl.semaphore_signal(barrier, inc=1, device_id={"seq": lax.rem(s + step, n_seq)}, device_id_type=MESH)

    @pl.when(t > 0)
    def _():
        pl.semaphore_signal(barrier, inc=1, device_id={"tp": t - 1}, device_id_type=MESH)

    @pl.when(t < n_tp - 1)
    def _():
        pl.semaphore_signal(barrier, inc=1, device_id={"tp": t + 1}, device_id_type=MESH)

    def weight_copy(k):
        return pltpu.make_async_copy(
            w_ref.at[:, pl.ds(pl.multiple_of(k * CHUNK, CHUNK), CHUNK)], wbuf.at[k], w_sem.at[k]
        )

    @pl.loop(0, plan.chunks)
    def _(k):
        weight_copy(k).start()

    for source in range(n_seq):
        pos_ref[source : source + 1, :] = flat_ref[:, source * rows : (source + 1) * rows]

    row_id = s * rows + iota((rows, 1), 0)
    gates = []
    for encoder in range(3):
        picked_logit = jnp.zeros((rows, 1), jnp.float32)
        for image in range(logit_ref.shape[0]):
            here = (row_id >= image * SIDE * SIDE) & (row_id < (image + 1) * SIDE * SIDE)
            picked_logit = jnp.where(here, logit_ref[image, encoder], picked_logit)
        gates.append(jax.nn.sigmoid(picked_logit))
    channel = t * plan.width + iota((rows, plan.width), 1)
    gate = jnp.where(channel < CLIP_C, gates[0], jnp.where(channel < CLIP_C + CNX_C, gates[1], gates[2]))
    gated = (feat_ref[...].astype(jnp.float32) * gate).astype(jnp.bfloat16)

    seq_rows = plan.rows_here * n_tp
    own_pos = pos_ref[pl.ds(s, 1), :]
    own_target = floor_div(own_pos, seq_rows)
    target_col = to_column(own_target)
    before = iota((rows, rows), 0) < iota((rows, rows), 1)
    own_slot = jnp.sum(
        jnp.where((target_col == own_target) & before, 1, 0), axis=0, keepdims=True
    )
    address = own_target * plan.cap_pad + own_slot
    choose = (address == iota((plan.slots, rows), 0)).astype(jnp.float32).astype(jnp.bfloat16)
    outgoing[...] = (
        jnp.dot(choose, gated, preferred_element_type=jnp.float32)
        .astype(jnp.bfloat16)
        .reshape(n_seq, plan.cap_pad, plan.width)
    )

    neighbours = jnp.where(t > 0, 1, 0) + jnp.where(t < n_tp - 1, 1, 0)
    pl.semaphore_wait(barrier, n_seq - 1 + neighbours)

    def exchange(step):
        peer = lax.rem(s + step, n_seq)
        return pltpu.make_async_remote_copy(
            src_ref=outgoing.at[peer],
            dst_ref=arrived.at[s],
            send_sem=x_send.at[step],
            recv_sem=x_recv.at[step],
            device_id={"seq": peer},
            device_id_type=MESH,
        )

    for step in range(1, n_seq):
        exchange(step).start()
    arrived[s] = outgoing[s]

    positions = pos_ref[...]
    offset = positions - s * seq_rows
    here = (offset >= 0) & (offset < seq_rows)
    earlier = before.astype(jnp.float32).astype(jnp.bfloat16)
    count = jnp.dot(
        here.astype(jnp.float32).astype(jnp.bfloat16), earlier, preferred_element_type=jnp.float32
    ).astype(jnp.int32)
    count = jnp.where(here, count, -1)
    slot_shape = (n_seq, plan.cap_pad, rows)
    hit = count.reshape(n_seq, 1, rows) == iota(slot_shape, 1)
    offset_of = jnp.where(hit, offset.reshape(n_seq, 1, rows) + 1, 0).reshape(plan.slots, rows)
    offset_col = jnp.sum(offset_of, axis=1, keepdims=True) - 1
    valid_col = offset_col >= 0
    sub_col = jnp.where(valid_col, floor_div(offset_col, plan.rows_here), -1)
    sub_row = to_row(sub_col)
    offset_row = to_row(offset_col)
    square = (plan.slots, plan.slots)
    rank_row = jnp.sum(
        jnp.where((sub_col == sub_row) & (iota(square, 0) < iota(square, 1)), 1, 0), axis=0, keepdims=True
    )
    packed_row = jnp.where(sub_row >= 0, sub_row * plan.sub_cap + rank_row, -1)
    picking = (
        (packed_row == iota((plan.packed, plan.slots), 0)).astype(jnp.float32).astype(jnp.bfloat16)
    )
    window = plan.window * 8
    base = lax.div(plan.sub_cap * t, 8) * 8
    mine = (packed_row == base + iota((window, plan.slots), 0)) & (sub_row == t)
    local = jnp.sum(
        jnp.where(mine, offset_row - t * plan.rows_here + 1, 0), axis=1, keepdims=True
    ) - 1
    row_ref[...] = to_row(local)

    for step in range(1, n_seq):
        exchange(step).wait_recv()
    picked[...] = jnp.dot(
        picking, arrived[...].reshape(plan.slots, plan.width), preferred_element_type=jnp.float32
    ).astype(jnp.bfloat16)

    def send_right(k, i):
        lo, hi = plan.right(i)
        return pltpu.make_async_remote_copy(
            src_ref=send_r.at[k, pl.ds(lo, hi - lo)],
            dst_ref=recv_r.at[k, pl.ds(lo, hi - lo)],
            send_sem=rs_send.at[k],
            recv_sem=rs_recv.at[k],
            device_id={"tp": lax.rem(t + 1, n_tp)},
            device_id_type=MESH,
        )

    def send_left(k, i):
        lo, hi = plan.left(i)
        return pltpu.make_async_remote_copy(
            src_ref=send_l.at[k, pl.ds(lo, hi - lo)],
            dst_ref=recv_l.at[k, pl.ds(lo, hi - lo)],
            send_sem=ls_send.at[k],
            recv_sem=ls_recv.at[k],
            device_id={"tp": lax.rem(t + n_tp - 1, n_tp)},
            device_id_type=MESH,
        )

    def pass_right(k, i):
        if i > 0:
            send_right(k, i - 1).wait_recv()
        if i < n_tp - 1:
            lo, hi = plan.right(i)
            block = part[k, lo:hi]
            if i > 0:
                block = block + recv_r[k, lo:hi].astype(jnp.float32)
            send_r[k, lo:hi] = block.astype(jnp.bfloat16)
            send_right(k, i).start()

    def pass_left(k, i):
        if i < n_tp - 1:
            send_left(k, i + 1).wait_recv()
        if i > 0:
            lo, hi = plan.left(i)
            block = part[k, lo:hi]
            if i < n_tp - 1:
                block = block + recv_l[k, lo:hi].astype(jnp.float32)
            send_l[k, lo:hi] = block.astype(jnp.bfloat16)
            send_left(k, i).start()

    def finish(k, i):
        first, last = plan.first[i], plan.last[i]
        total = part[k, first:last]
        if i > 0:
            total = total + recv_r[k, first:last].astype(jnp.float32)
        if i < n_tp - 1:
            total = total + recv_l[k, first:last].astype(jnp.float32)
        columns = pl.ds(pl.multiple_of(k * CHUNK, CHUNK), CHUNK)
        out_ref[0 : last - first, :, columns] = total.astype(jnp.bfloat16)
        if last - first < plan.window:
            out_ref[last - first :, :, columns] = jnp.zeros(
                (plan.window - (last - first), 8, CHUNK), jnp.bfloat16
            )

    lags = [min(LAG * (abs(2 * i - n_tp + 1) + 1) // 2, plan.chunks) for i in range(n_tp)]

    @pl.loop(0, plan.chunks + max(lags))
    def _(step):
        @pl.when(step < plan.chunks)
        def _():
            weight_copy(step).wait()
            result = jnp.dot(picked[...], wbuf[step], preferred_element_type=jnp.float32)
            part[step] = result.reshape(plan.groups, 8, CHUNK)
            for i in range(n_tp):

                @pl.when(t == i)
                def _(i=i):
                    (pass_right if 2 * i < n_tp else pass_left)(step, i)

        for i in range(n_tp):

            @pl.when((t == i) & (step >= lags[i]) & (step < plan.chunks + lags[i]))
            def _(i=i):
                (pass_left if 2 * i < n_tp else pass_right)(step - lags[i], i)
                finish(step - lags[i], i)

    for i in range(n_tp):

        @pl.when(t == i)
        def _(i=i):
            @pl.loop(0, plan.chunks)
            def _(k):
                if i < n_tp - 1:
                    send_right(k, i).wait_send()
                if i > 0:
                    send_left(k, i).wait_send()

    for step in range(1, n_seq):
        exchange(step).wait_send()


def place_kernel(row_ref, summed_ref, text_ref, out_ref):
    block = text_ref.shape[0]
    window = summed_ref.shape[0] * 8
    local = row_ref[0:1, :] - pl.program_id(0) * block
    hits = (local == iota((block, window), 0)).astype(jnp.float32)
    filled = jnp.sum(hits, axis=1, keepdims=True) > 0.5
    values = summed_ref[...].reshape(window, text_ref.shape[1])
    placed = jnp.dot(hits.astype(jnp.bfloat16), values, preferred_element_type=jnp.float32)
    out_ref[...] = jnp.where(filled, placed.astype(jnp.bfloat16), text_ref[...])


def shards(features, gate_logits, proj_weight, positions, text):
    n_seq, n_tp = lax.axis_size("seq"), lax.axis_size("tp")
    rows, width = features.shape
    depth = proj_weight.shape[1]
    rows_here = text.shape[0]
    plan = Plan(n_seq, n_tp, rows, width, depth, rows_here)
    vmem = pl.BlockSpec(memory_space=pltpu.VMEM)
    moving = pltpu.VMEM((plan.chunks, plan.groups, 8, CHUNK), jnp.bfloat16)
    summed, local_rows = pl.pallas_call(
        functools.partial(join_kernel, plan),
        out_shape=(
            jax.ShapeDtypeStruct((plan.window, 8, depth), jnp.bfloat16),
            jax.ShapeDtypeStruct((1, plan.window * 8), jnp.int32),
        ),
        in_specs=[
            vmem,
            pl.BlockSpec(memory_space=pltpu.SMEM),
            vmem,
            pl.BlockSpec(memory_space=pl.ANY),
        ],
        out_specs=(vmem, vmem),
        scratch_shapes=[
            pltpu.VMEM((n_seq, rows), jnp.int32),
            pltpu.VMEM((plan.chunks, width, CHUNK), jnp.bfloat16),
            pltpu.VMEM((n_seq, plan.cap_pad, width), jnp.bfloat16),
            pltpu.VMEM((n_seq, plan.cap_pad, width), jnp.bfloat16),
            pltpu.VMEM((plan.packed, width), jnp.bfloat16),
            pltpu.VMEM((plan.chunks, plan.groups, 8, CHUNK), jnp.float32),
            moving, moving, moving, moving,
            pltpu.SemaphoreType.DMA((plan.chunks,)),
            pltpu.SemaphoreType.DMA((n_seq,)),
            pltpu.SemaphoreType.DMA((n_seq,)),
            pltpu.SemaphoreType.DMA((plan.chunks,)),
            pltpu.SemaphoreType.DMA((plan.chunks,)),
            pltpu.SemaphoreType.DMA((plan.chunks,)),
            pltpu.SemaphoreType.DMA((plan.chunks,)),
        ],
        compiler_params=pltpu.CompilerParams(
            collective_id=0, has_side_effects=True, vmem_limit_bytes=44 * 1024 * 1024
        ),
        name="join",
    )(positions.reshape(1, n_seq * rows), gate_logits, features, proj_weight)

    window = plan.window * 8
    block = 64 if rows_here % 64 == 0 else rows_here
    return pl.pallas_call(
        place_kernel,
        grid=(rows_here // block,),
        out_shape=jax.ShapeDtypeStruct(text.shape, text.dtype),
        in_specs=[
            pl.BlockSpec((1, window), lambda i: (0, 0)),
            pl.BlockSpec((plan.window, 8, depth), lambda i: (0, 0, 0)),
            pl.BlockSpec((block, depth), lambda i: (i, 0)),
        ],
        out_specs=pl.BlockSpec((block, depth), lambda i: (i, 0)),
        compiler_params=pltpu.CompilerParams(vmem_limit_bytes=24 * 1024 * 1024),
        name="place",
    )(local_rows, summed, text)


def solution(mesh):
    return jax.shard_map(
        shards,
        mesh=mesh,
        in_specs=(P("seq", "tp"), P(), P("tp", None), P(), P(("seq", "tp"), None)),
        out_specs=P(("seq", "tp"), None),
        check_vma=False,
    )
```

```python
import functools

import jax
import jax.numpy as jnp
from jax import lax
from jax.experimental import pallas as pl
from jax.experimental.pallas import tpu as pltpu
from jax.sharding import PartitionSpec as P

CLIP_C = 1024
CNX_C = 3072
SIDE = 24
MESH = pl.DeviceIdType.MESH
CHUNK = 1024
LAG = 4


def up(value, unit):
    return -(-value // unit) * unit


def iota(shape, dim):
    return lax.broadcasted_iota(jnp.int32, shape, dim)


def floor_div(value, unit):
    return ((value.astype(jnp.float32) + 0.5) * (1.0 / unit)).astype(jnp.int32)


def to_row(column):
    size = column.shape[0]
    eye = iota((size, size), 0) == iota((size, size), 1)
    return jnp.sum(jnp.where(eye, column, 0), axis=0, keepdims=True)


def to_column(row):
    size = row.shape[1]
    eye = iota((size, size), 0) == iota((size, size), 1)
    return jnp.sum(jnp.where(eye, row, 0), axis=1, keepdims=True)


class Plan:
    def __init__(self, n_seq, n_tp, rows, width, depth, rows_here):
        self.n_seq, self.n_tp, self.rows, self.width = n_seq, n_tp, rows, width
        self.depth, self.rows_here = depth, rows_here
        self.cap = -(-rows // n_seq)
        self.cap_pad = up(self.cap, 16)
        self.slots = n_seq * self.cap_pad
        self.sub_cap = -(-(n_seq * self.cap) // n_tp)
        self.packed = up(n_tp * self.sub_cap, 8)
        self.groups = self.packed // 8
        self.chunks = depth // CHUNK
        self.first = [self.sub_cap * t // 8 for t in range(n_tp)]
        self.last = [-(-self.sub_cap * (t + 1) // 8) for t in range(n_tp)]
        self.window = max(b - a for a, b in zip(self.first, self.last))

    def right(self, dest):
        return self.first[dest], self.first[dest + 1] if dest < self.n_tp - 1 else self.groups

    def left(self, dest):
        return self.last[dest - 1] if dest > 0 else 0, self.last[dest]


def join_kernel(
    plan, flat_ref, logit_ref, feat_ref, w_ref,
    out_ref, row_ref,
    pos_ref, wbuf, outgoing, arrived, picked, part, send_r, send_l, recv_r, recv_l,
    w_sem, x_send, x_recv, rs_send, rs_recv, ls_send, ls_recv,
):
    n_seq, n_tp, rows = plan.n_seq, plan.n_tp, plan.rows
    s = lax.axis_index("seq")
    t = lax.axis_index("tp")

    barrier = pltpu.get_barrier_semaphore()
    for step in range(1, n_seq):
        pl.semaphore_signal(barrier, inc=1, device_id={"seq": lax.rem(s + step, n_seq)}, device_id_type=MESH)

    @pl.when(t > 0)
    def _():
        pl.semaphore_signal(barrier, inc=1, device_id={"tp": t - 1}, device_id_type=MESH)

    @pl.when(t < n_tp - 1)
    def _():
        pl.semaphore_signal(barrier, inc=1, device_id={"tp": t + 1}, device_id_type=MESH)

    def weight_copy(k):
        return pltpu.make_async_copy(
            w_ref.at[:, pl.ds(pl.multiple_of(k * CHUNK, CHUNK), CHUNK)], wbuf.at[k], w_sem.at[k]
        )

    @pl.loop(0, plan.chunks)
    def _(k):
        weight_copy(k).start()

    for source in range(n_seq):
        pos_ref[source : source + 1, :] = flat_ref[:, source * rows : (source + 1) * rows]

    row_id = s * rows + iota((rows, 1), 0)
    gates = []
    for encoder in range(3):
        picked_logit = jnp.zeros((rows, 1), jnp.float32)
        for image in range(logit_ref.shape[0]):
            here = (row_id >= image * SIDE * SIDE) & (row_id < (image + 1) * SIDE * SIDE)
            picked_logit = jnp.where(here, logit_ref[image, encoder], picked_logit)
        gates.append(jax.nn.sigmoid(picked_logit))
    channel = t * plan.width + iota((rows, plan.width), 1)
    gate = jnp.where(channel < CLIP_C, gates[0], jnp.where(channel < CLIP_C + CNX_C, gates[1], gates[2]))
    gated = (feat_ref[...].astype(jnp.float32) * gate).astype(jnp.bfloat16)

    seq_rows = plan.rows_here * n_tp
    own_pos = pos_ref[pl.ds(s, 1), :]
    own_target = floor_div(own_pos, seq_rows)
    target_col = to_column(own_target)
    before = iota((rows, rows), 0) < iota((rows, rows), 1)
    own_slot = jnp.sum(
        jnp.where((target_col == own_target) & before, 1, 0), axis=0, keepdims=True
    )
    address = own_target * plan.cap_pad + own_slot
    choose = (address == iota((plan.slots, rows), 0)).astype(jnp.float32).astype(jnp.bfloat16)
    outgoing[...] = (
        jnp.dot(choose, gated, preferred_element_type=jnp.float32)
        .astype(jnp.bfloat16)
        .reshape(n_seq, plan.cap_pad, plan.width)
    )

    neighbours = jnp.where(t > 0, 1, 0) + jnp.where(t < n_tp - 1, 1, 0)
    pl.semaphore_wait(barrier, n_seq - 1 + neighbours)

    def exchange(step):
        peer = lax.rem(s + step, n_seq)
        return pltpu.make_async_remote_copy(
            src_ref=outgoing.at[peer],
            dst_ref=arrived.at[s],
            send_sem=x_send.at[step],
            recv_sem=x_recv.at[step],
            device_id={"seq": peer},
            device_id_type=MESH,
        )

    for step in range(1, n_seq):
        exchange(step).start()
    arrived[s] = outgoing[s]

    positions = pos_ref[...]
    offset = positions - s * seq_rows
    here = (offset >= 0) & (offset < seq_rows)
    earlier = before.astype(jnp.float32).astype(jnp.bfloat16)
    count = jnp.dot(
        here.astype(jnp.float32).astype(jnp.bfloat16), earlier, preferred_element_type=jnp.float32
    ).astype(jnp.int32)
    count = jnp.where(here, count, -1)
    slot_shape = (n_seq, plan.cap_pad, rows)
    hit = count.reshape(n_seq, 1, rows) == iota(slot_shape, 1)
    offset_of = jnp.where(hit, offset.reshape(n_seq, 1, rows) + 1, 0).reshape(plan.slots, rows)
    offset_col = jnp.sum(offset_of, axis=1, keepdims=True) - 1
    valid_col = offset_col >= 0
    sub_col = jnp.where(valid_col, floor_div(offset_col, plan.rows_here), -1)
    sub_row = to_row(sub_col)
    offset_row = to_row(offset_col)
    square = (plan.slots, plan.slots)
    rank_row = jnp.sum(
        jnp.where((sub_col == sub_row) & (iota(square, 0) < iota(square, 1)), 1, 0), axis=0, keepdims=True
    )
    packed_row = jnp.where(sub_row >= 0, sub_row * plan.sub_cap + rank_row, -1)
    picking = (
        (packed_row == iota((plan.packed, plan.slots), 0)).astype(jnp.float32).astype(jnp.bfloat16)
    )
    window = plan.window * 8
    base = lax.div(plan.sub_cap * t, 8) * 8
    mine = (packed_row == base + iota((window, plan.slots), 0)) & (sub_row == t)
    local = jnp.sum(
        jnp.where(mine, offset_row - t * plan.rows_here + 1, 0), axis=1, keepdims=True
    ) - 1
    row_ref[...] = to_row(local)

    for step in range(1, n_seq):
        exchange(step).wait_recv()
    picked[...] = jnp.dot(
        picking, arrived[...].reshape(plan.slots, plan.width), preferred_element_type=jnp.float32
    ).astype(jnp.bfloat16)

    chunks = plan.chunks

    def send_right(k, dest):
        lo, hi = plan.right(dest)
        return pltpu.make_async_remote_copy(
            src_ref=send_r.at[k, pl.ds(lo, hi - lo)],
            dst_ref=recv_r.at[k, pl.ds(lo, hi - lo)],
            send_sem=rs_send.at[dest * chunks + k],
            recv_sem=rs_recv.at[dest * chunks + k],
            device_id={"tp": lax.rem(t + 1, n_tp)},
            device_id_type=MESH,
        )

    def send_left(k, dest):
        lo, hi = plan.left(dest)
        return pltpu.make_async_remote_copy(
            src_ref=send_l.at[k, pl.ds(lo, hi - lo)],
            dst_ref=recv_l.at[k, pl.ds(lo, hi - lo)],
            send_sem=ls_send.at[dest * chunks + k],
            recv_sem=ls_recv.at[dest * chunks + k],
            device_id={"tp": lax.rem(t + n_tp - 1, n_tp)},
            device_id_type=MESH,
        )

    def pass_right(i, phase, k):
        dest = n_tp - 1 - phase
        if dest < i:
            return
        if i > 0:
            send_right(k, dest).wait_recv()
        if dest > i:
            lo, hi = plan.right(dest)
            block = part[k, lo:hi]
            if i > 0:
                block = block + recv_r[k, lo:hi].astype(jnp.float32)
            send_r[k, lo:hi] = block.astype(jnp.bfloat16)
            send_right(k, dest).start()

    def pass_left(i, phase, k):
        dest = phase
        if dest > i:
            return
        if i < n_tp - 1:
            send_left(k, dest).wait_recv()
        if dest < i:
            lo, hi = plan.left(dest)
            block = part[k, lo:hi]
            if i < n_tp - 1:
                block = block + recv_l[k, lo:hi].astype(jnp.float32)
            send_l[k, lo:hi] = block.astype(jnp.bfloat16)
            send_left(k, dest).start()

    def finish(i, phase, k):
        first, last = plan.first[i], plan.last[i]
        total = part[k, first:last]
        if i > 0:
            total = total + recv_r[k, first:last].astype(jnp.float32)
        if i < n_tp - 1:
            total = total + recv_l[k, first:last].astype(jnp.float32)
        columns = pl.ds(pl.multiple_of(k * CHUNK, CHUNK), CHUNK)
        out_ref[0 : last - first, :, columns] = total.astype(jnp.bfloat16)
        if last - first < plan.window:
            out_ref[last - first :, :, columns] = jnp.zeros(
                (plan.window - (last - first), 8, CHUNK), jnp.bfloat16
            )

    def shifted(i, block, k, offset, count, act):
        skip, part_of = divmod(offset, chunks)
        phase = block - skip
        if 0 <= phase < count:

            @pl.when(k >= part_of)
            def _():
                act(i, phase, k - part_of)

        if part_of > 0 and 0 <= phase - 1 < count:

            @pl.when(k < part_of)
            def _():
                act(i, phase - 1, k - part_of + chunks)

    def schedule(i):
        near_right = 2 * i < n_tp
        end = i in (0, n_tp - 1)
        hops = (abs(2 * i - n_tp + 1) + 1) // 2
        lag = (n_tp - 1) * chunks if end else min(LAG * hops, chunks)
        right_last, left_last = n_tp - 1 - i, i
        near_last, far_last = (right_last, left_last) if near_right else (left_last, right_last)
        done = max(0 if end else near_last * chunks, far_last * chunks + lag)
        return near_right, lag, far_last + 1, done

    def block_step(i, block, k):
        near_right, lag, far_count, done = schedule(i)
        near, far = (pass_right, pass_left) if near_right else (pass_left, pass_right)
        if block < n_tp:
            near(i, block, k)
        shifted(i, block, k, lag, far_count, far)
        shifted(i, block, k, done, 1, finish)

    @pl.loop(0, chunks)
    def _(k):
        weight_copy(k).wait()
        result = jnp.dot(picked[...], wbuf[k], preferred_element_type=jnp.float32)
        part[k] = result.reshape(plan.groups, 8, CHUNK)
        for i in range(n_tp):

            @pl.when(t == i)
            def _(i=i):
                block_step(i, 0, k)

    for i in range(n_tp):

        @pl.when(t == i)
        def _(i=i):
            done = schedule(i)[3]
            for block in range(1, -(-done // chunks) + 1):

                @pl.loop(0, chunks)
                def _(k):
                    block_step(i, block, k)

            @pl.loop(0, chunks)
            def _(k):
                for dest in range(i + 1, n_tp):
                    send_right(k, dest).wait_send()
                for dest in range(i):
                    send_left(k, dest).wait_send()

    for step in range(1, n_seq):
        exchange(step).wait_send()


def place_kernel(row_ref, summed_ref, text_ref, out_ref):
    block = text_ref.shape[0]
    window = summed_ref.shape[0] * 8
    local = row_ref[0:1, :] - pl.program_id(0) * block
    hits = (local == iota((block, window), 0)).astype(jnp.float32)
    filled = jnp.sum(hits, axis=1, keepdims=True) > 0.5
    values = summed_ref[...].reshape(window, text_ref.shape[1])
    placed = jnp.dot(hits.astype(jnp.bfloat16), values, preferred_element_type=jnp.float32)
    out_ref[...] = jnp.where(filled, placed.astype(jnp.bfloat16), text_ref[...])


def shards(features, gate_logits, proj_weight, positions, text):
    n_seq, n_tp = lax.axis_size("seq"), lax.axis_size("tp")
    rows, width = features.shape
    depth = proj_weight.shape[1]
    rows_here = text.shape[0]
    plan = Plan(n_seq, n_tp, rows, width, depth, rows_here)
    vmem = pl.BlockSpec(memory_space=pltpu.VMEM)
    moving = pltpu.VMEM((plan.chunks, plan.groups, 8, CHUNK), jnp.bfloat16)
    summed, local_rows = pl.pallas_call(
        functools.partial(join_kernel, plan),
        out_shape=(
            jax.ShapeDtypeStruct((plan.window, 8, depth), jnp.bfloat16),
            jax.ShapeDtypeStruct((1, plan.window * 8), jnp.int32),
        ),
        in_specs=[
            vmem,
            pl.BlockSpec(memory_space=pltpu.SMEM),
            vmem,
            pl.BlockSpec(memory_space=pl.ANY),
        ],
        out_specs=(vmem, vmem),
        scratch_shapes=[
            pltpu.VMEM((n_seq, rows), jnp.int32),
            pltpu.VMEM((plan.chunks, width, CHUNK), jnp.bfloat16),
            pltpu.VMEM((n_seq, plan.cap_pad, width), jnp.bfloat16),
            pltpu.VMEM((n_seq, plan.cap_pad, width), jnp.bfloat16),
            pltpu.VMEM((plan.packed, width), jnp.bfloat16),
            pltpu.VMEM((plan.chunks, plan.groups, 8, CHUNK), jnp.float32),
            moving, moving, moving, moving,
            pltpu.SemaphoreType.DMA((plan.chunks,)),
            pltpu.SemaphoreType.DMA((n_seq,)),
            pltpu.SemaphoreType.DMA((n_seq,)),
            pltpu.SemaphoreType.DMA((n_tp * plan.chunks,)),
            pltpu.SemaphoreType.DMA((n_tp * plan.chunks,)),
            pltpu.SemaphoreType.DMA((n_tp * plan.chunks,)),
            pltpu.SemaphoreType.DMA((n_tp * plan.chunks,)),
        ],
        compiler_params=pltpu.CompilerParams(
            collective_id=0, has_side_effects=True, vmem_limit_bytes=44 * 1024 * 1024
        ),
        name="join",
    )(positions.reshape(1, n_seq * rows), gate_logits, features, proj_weight)

    window = plan.window * 8
    block = 64 if rows_here % 64 == 0 else rows_here
    return pl.pallas_call(
        place_kernel,
        grid=(rows_here // block,),
        out_shape=jax.ShapeDtypeStruct(text.shape, text.dtype),
        in_specs=[
            pl.BlockSpec((1, window), lambda i: (0, 0)),
            pl.BlockSpec((plan.window, 8, depth), lambda i: (0, 0, 0)),
            pl.BlockSpec((block, depth), lambda i: (i, 0)),
        ],
        out_specs=pl.BlockSpec((block, depth), lambda i: (i, 0)),
        compiler_params=pltpu.CompilerParams(vmem_limit_bytes=24 * 1024 * 1024),
        name="place",
    )(local_rows, summed, text)


def solution(mesh):
    return jax.shard_map(
        shards,
        mesh=mesh,
        in_specs=(P("seq", "tp"), P(), P("tp", None), P(), P(("seq", "tp"), None)),
        out_specs=P(("seq", "tp"), None),
        check_vma=False,
    )
```

```python
import functools

import jax
import jax.numpy as jnp
from jax import lax
from jax.experimental import pallas as pl
from jax.experimental.pallas import tpu as pltpu
from jax.sharding import PartitionSpec as P

CLIP_C = 1024
CNX_C = 3072
SIDE = 24
MESH = pl.DeviceIdType.MESH
CHUNK = 1024
LAG = 4


def up(value, unit):
    return -(-value // unit) * unit


def iota(shape, dim):
    return lax.broadcasted_iota(jnp.int32, shape, dim)


def floor_div(value, unit):
    return ((value.astype(jnp.float32) + 0.5) * (1.0 / unit)).astype(jnp.int32)


def to_row(column):
    size = column.shape[0]
    eye = iota((size, size), 0) == iota((size, size), 1)
    return jnp.sum(jnp.where(eye, column, 0), axis=0, keepdims=True)


def to_column(row):
    size = row.shape[1]
    eye = iota((size, size), 0) == iota((size, size), 1)
    return jnp.sum(jnp.where(eye, row, 0), axis=1, keepdims=True)


class Plan:
    def __init__(self, n_seq, n_tp, rows, width, depth, rows_here):
        self.n_seq, self.n_tp, self.rows, self.width = n_seq, n_tp, rows, width
        self.depth, self.rows_here = depth, rows_here
        self.cap = -(-rows // n_seq)
        self.cap_pad = up(self.cap, 16)
        self.slots = n_seq * self.cap_pad
        self.sub_cap = -(-(n_seq * self.cap) // n_tp)
        self.packed = up(n_tp * self.sub_cap, 8)
        self.groups = self.packed // 8
        self.chunks = depth // CHUNK
        self.first = [self.sub_cap * t // 8 for t in range(n_tp)]
        self.last = [-(-self.sub_cap * (t + 1) // 8) for t in range(n_tp)]
        self.window = max(b - a for a, b in zip(self.first, self.last))

    def right(self, dest):
        return self.first[dest], self.first[dest + 1] if dest < self.n_tp - 1 else self.groups

    def left(self, dest):
        return self.last[dest - 1] if dest > 0 else 0, self.last[dest]


def join_kernel(
    plan, flat_ref, logit_hbm, feat_hbm, w_ref,
    out_ref, row_ref,
    logit_ref, feat_ref, in_sem, pos_ref, wbuf, outgoing, arrived, picked, part, send_r, send_l, recv_r, recv_l,
    w_sem, x_send, x_recv, rs_send, rs_recv, ls_send, ls_recv,
):
    n_seq, n_tp, rows = plan.n_seq, plan.n_tp, plan.rows
    s = lax.axis_index("seq")
    t = lax.axis_index("tp")

    feat_copy = pltpu.make_async_copy(feat_hbm, feat_ref, in_sem.at[0])
    logit_copy = pltpu.make_async_copy(logit_hbm, logit_ref, in_sem.at[1])
    feat_copy.start()
    logit_copy.start()

    barrier = pltpu.get_barrier_semaphore()
    for step in range(1, n_seq):
        pl.semaphore_signal(barrier, inc=1, device_id={"seq": lax.rem(s + step, n_seq)}, device_id_type=MESH)

    @pl.when(t > 0)
    def _():
        pl.semaphore_signal(barrier, inc=1, device_id={"tp": t - 1}, device_id_type=MESH)

    @pl.when(t < n_tp - 1)
    def _():
        pl.semaphore_signal(barrier, inc=1, device_id={"tp": t + 1}, device_id_type=MESH)

    def weight_copy(k):
        return pltpu.make_async_copy(
            w_ref.at[:, pl.ds(pl.multiple_of(k * CHUNK, CHUNK), CHUNK)], wbuf.at[k], w_sem.at[k]
        )

    @pl.loop(0, plan.chunks)
    def _(k):
        weight_copy(k).start()

    for source in range(n_seq):
        pos_ref[source : source + 1, :] = flat_ref[:, source * rows : (source + 1) * rows]

    seq_rows = plan.rows_here * n_tp
    own_pos = pos_ref[pl.ds(s, 1), :]
    own_target = floor_div(own_pos, seq_rows)
    target_col = to_column(own_target)
    before = iota((rows, rows), 0) < iota((rows, rows), 1)
    own_slot = jnp.sum(
        jnp.where((target_col == own_target) & before, 1, 0), axis=0, keepdims=True
    )
    address = own_target * plan.cap_pad + own_slot
    choose = (address == iota((plan.slots, rows), 0)).astype(jnp.float32).astype(jnp.bfloat16)

    logit_copy.wait()
    feat_copy.wait()
    row_id = s * rows + iota((rows, 1), 0)
    gates = []
    for encoder in range(3):
        picked_logit = jnp.zeros((rows, 1), jnp.float32)
        for image in range(logit_ref.shape[0]):
            here = (row_id >= image * SIDE * SIDE) & (row_id < (image + 1) * SIDE * SIDE)
            picked_logit = jnp.where(here, logit_ref[image, encoder], picked_logit)
        gates.append(jax.nn.sigmoid(picked_logit))
    channel = t * plan.width + iota((rows, plan.width), 1)
    gate = jnp.where(channel < CLIP_C, gates[0], jnp.where(channel < CLIP_C + CNX_C, gates[1], gates[2]))
    gated = (feat_ref[...].astype(jnp.float32) * gate).astype(jnp.bfloat16)
    outgoing[...] = (
        jnp.dot(choose, gated, preferred_element_type=jnp.float32)
        .astype(jnp.bfloat16)
        .reshape(n_seq, plan.cap_pad, plan.width)
    )

    neighbours = jnp.where(t > 0, 1, 0) + jnp.where(t < n_tp - 1, 1, 0)
    pl.semaphore_wait(barrier, n_seq - 1 + neighbours)

    def exchange(step):
        peer = lax.rem(s + step, n_seq)
        return pltpu.make_async_remote_copy(
            src_ref=outgoing.at[peer],
            dst_ref=arrived.at[s],
            send_sem=x_send.at[step],
            recv_sem=x_recv.at[step],
            device_id={"seq": peer},
            device_id_type=MESH,
        )

    for step in range(1, n_seq):
        exchange(step).start()
    arrived[s] = outgoing[s]

    positions = pos_ref[...]
    offset = positions - s * seq_rows
    here = (offset >= 0) & (offset < seq_rows)
    earlier = before.astype(jnp.float32).astype(jnp.bfloat16)
    count = jnp.dot(
        here.astype(jnp.float32).astype(jnp.bfloat16), earlier, preferred_element_type=jnp.float32
    ).astype(jnp.int32)
    count = jnp.where(here, count, -1)
    slot_shape = (n_seq, plan.cap_pad, rows)
    hit = count.reshape(n_seq, 1, rows) == iota(slot_shape, 1)
    offset_of = jnp.where(hit, offset.reshape(n_seq, 1, rows) + 1, 0).reshape(plan.slots, rows)
    offset_col = jnp.sum(offset_of, axis=1, keepdims=True) - 1
    valid_col = offset_col >= 0
    sub_col = jnp.where(valid_col, floor_div(offset_col, plan.rows_here), -1)
    sub_row = to_row(sub_col)
    offset_row = to_row(offset_col)
    square = (plan.slots, plan.slots)
    rank_row = jnp.sum(
        jnp.where((sub_col == sub_row) & (iota(square, 0) < iota(square, 1)), 1, 0), axis=0, keepdims=True
    )
    packed_row = jnp.where(sub_row >= 0, sub_row * plan.sub_cap + rank_row, -1)
    picking = (
        (packed_row == iota((plan.packed, plan.slots), 0)).astype(jnp.float32).astype(jnp.bfloat16)
    )
    window = plan.window * 8
    base = lax.div(plan.sub_cap * t, 8) * 8
    mine = (packed_row == base + iota((window, plan.slots), 0)) & (sub_row == t)
    local = jnp.sum(
        jnp.where(mine, offset_row - t * plan.rows_here + 1, 0), axis=1, keepdims=True
    ) - 1
    row_ref[...] = to_row(local)

    for step in range(1, n_seq):
        exchange(step).wait_recv()
    picked[...] = jnp.dot(
        picking, arrived[...].reshape(plan.slots, plan.width), preferred_element_type=jnp.float32
    ).astype(jnp.bfloat16)

    chunks = plan.chunks

    def send_right(k, dest):
        lo, hi = plan.right(dest)
        return pltpu.make_async_remote_copy(
            src_ref=send_r.at[k, pl.ds(lo, hi - lo)],
            dst_ref=recv_r.at[k, pl.ds(lo, hi - lo)],
            send_sem=rs_send.at[dest * chunks + k],
            recv_sem=rs_recv.at[dest * chunks + k],
            device_id={"tp": lax.rem(t + 1, n_tp)},
            device_id_type=MESH,
        )

    def send_left(k, dest):
        lo, hi = plan.left(dest)
        return pltpu.make_async_remote_copy(
            src_ref=send_l.at[k, pl.ds(lo, hi - lo)],
            dst_ref=recv_l.at[k, pl.ds(lo, hi - lo)],
            send_sem=ls_send.at[dest * chunks + k],
            recv_sem=ls_recv.at[dest * chunks + k],
            device_id={"tp": lax.rem(t + n_tp - 1, n_tp)},
            device_id_type=MESH,
        )

    def pass_right(i, phase, k):
        dest = n_tp - 1 - phase
        if dest < i:
            return
        if i > 0:
            send_right(k, dest).wait_recv()
        if dest > i:
            lo, hi = plan.right(dest)
            block = part[k, lo:hi]
            if i > 0:
                block = block + recv_r[k, lo:hi].astype(jnp.float32)
            send_r[k, lo:hi] = block.astype(jnp.bfloat16)
            send_right(k, dest).start()

    def pass_left(i, phase, k):
        dest = phase
        if dest > i:
            return
        if i < n_tp - 1:
            send_left(k, dest).wait_recv()
        if dest < i:
            lo, hi = plan.left(dest)
            block = part[k, lo:hi]
            if i < n_tp - 1:
                block = block + recv_l[k, lo:hi].astype(jnp.float32)
            send_l[k, lo:hi] = block.astype(jnp.bfloat16)
            send_left(k, dest).start()

    def finish(i, phase, k):
        first, last = plan.first[i], plan.last[i]
        total = part[k, first:last]
        if i > 0:
            total = total + recv_r[k, first:last].astype(jnp.float32)
        if i < n_tp - 1:
            total = total + recv_l[k, first:last].astype(jnp.float32)
        columns = pl.ds(pl.multiple_of(k * CHUNK, CHUNK), CHUNK)
        out_ref[0 : last - first, :, columns] = total.astype(jnp.bfloat16)
        if last - first < plan.window:
            out_ref[last - first :, :, columns] = jnp.zeros(
                (plan.window - (last - first), 8, CHUNK), jnp.bfloat16
            )

    def shifted(i, block, k, offset, count, act):
        skip, part_of = divmod(offset, chunks)
        phase = block - skip
        if 0 <= phase < count:

            @pl.when(k >= part_of)
            def _():
                act(i, phase, k - part_of)

        if part_of > 0 and 0 <= phase - 1 < count:

            @pl.when(k < part_of)
            def _():
                act(i, phase - 1, k - part_of + chunks)

    def schedule(i):
        near_right = 2 * i < n_tp
        end = i in (0, n_tp - 1)
        hops = (abs(2 * i - n_tp + 1) + 1) // 2
        lag = (n_tp - 1) * chunks if end else min(LAG * hops, chunks)
        right_last, left_last = n_tp - 1 - i, i
        near_last, far_last = (right_last, left_last) if near_right else (left_last, right_last)
        done = max(0 if end else near_last * chunks, far_last * chunks + lag)
        return near_right, lag, far_last + 1, done

    def block_step(i, block, k):
        near_right, lag, far_count, done = schedule(i)
        near, far = (pass_right, pass_left) if near_right else (pass_left, pass_right)
        if block < n_tp:
            near(i, block, k)
        shifted(i, block, k, lag, far_count, far)
        shifted(i, block, k, done, 1, finish)

    @pl.loop(0, chunks)
    def _(k):
        weight_copy(k).wait()
        result = jnp.dot(picked[...], wbuf[k], preferred_element_type=jnp.float32)
        part[k] = result.reshape(plan.groups, 8, CHUNK)
        for i in range(n_tp):

            @pl.when(t == i)
            def _(i=i):
                block_step(i, 0, k)

    for i in range(n_tp):

        @pl.when(t == i)
        def _(i=i):
            done = schedule(i)[3]
            for block in range(1, -(-done // chunks) + 1):

                @pl.loop(0, chunks)
                def _(k):
                    block_step(i, block, k)

            @pl.loop(0, chunks)
            def _(k):
                for dest in range(i + 1, n_tp):
                    send_right(k, dest).wait_send()
                for dest in range(i):
                    send_left(k, dest).wait_send()

    for step in range(1, n_seq):
        exchange(step).wait_send()


def place_kernel(row_ref, summed_ref, text_ref, out_ref):
    block = text_ref.shape[0]
    window = summed_ref.shape[0] * 8
    local = row_ref[0:1, :] - pl.program_id(0) * block
    hits = (local == iota((block, window), 0)).astype(jnp.float32)
    filled = jnp.sum(hits, axis=1, keepdims=True) > 0.5
    values = summed_ref[...].reshape(window, text_ref.shape[1])
    placed = jnp.dot(hits.astype(jnp.bfloat16), values, preferred_element_type=jnp.float32)
    out_ref[...] = jnp.where(filled, placed.astype(jnp.bfloat16), text_ref[...])


def shards(features, gate_logits, proj_weight, positions, text):
    n_seq, n_tp = lax.axis_size("seq"), lax.axis_size("tp")
    rows, width = features.shape
    depth = proj_weight.shape[1]
    rows_here = text.shape[0]
    plan = Plan(n_seq, n_tp, rows, width, depth, rows_here)
    vmem = pl.BlockSpec(memory_space=pltpu.VMEM)
    moving = pltpu.VMEM((plan.chunks, plan.groups, 8, CHUNK), jnp.bfloat16)
    summed, local_rows = pl.pallas_call(
        functools.partial(join_kernel, plan),
        out_shape=(
            jax.ShapeDtypeStruct((plan.window, 8, depth), jnp.bfloat16),
            jax.ShapeDtypeStruct((1, plan.window * 8), jnp.int32),
        ),
        in_specs=[
            vmem,
            pl.BlockSpec(memory_space=pltpu.HBM),
            pl.BlockSpec(memory_space=pltpu.HBM),
            pl.BlockSpec(memory_space=pl.ANY),
        ],
        out_specs=(vmem, vmem),
        scratch_shapes=[
            pltpu.SMEM(gate_logits.shape, jnp.float32),
            pltpu.VMEM((rows, width), jnp.bfloat16),
            pltpu.SemaphoreType.DMA((2,)),
            pltpu.VMEM((n_seq, rows), jnp.int32),
            pltpu.VMEM((plan.chunks, width, CHUNK), jnp.bfloat16),
            pltpu.VMEM((n_seq, plan.cap_pad, width), jnp.bfloat16),
            pltpu.VMEM((n_seq, plan.cap_pad, width), jnp.bfloat16),
            pltpu.VMEM((plan.packed, width), jnp.bfloat16),
            pltpu.VMEM((plan.chunks, plan.groups, 8, CHUNK), jnp.float32),
            moving, moving, moving, moving,
            pltpu.SemaphoreType.DMA((plan.chunks,)),
            pltpu.SemaphoreType.DMA((n_seq,)),
            pltpu.SemaphoreType.DMA((n_seq,)),
            pltpu.SemaphoreType.DMA((n_tp * plan.chunks,)),
            pltpu.SemaphoreType.DMA((n_tp * plan.chunks,)),
            pltpu.SemaphoreType.DMA((n_tp * plan.chunks,)),
            pltpu.SemaphoreType.DMA((n_tp * plan.chunks,)),
        ],
        compiler_params=pltpu.CompilerParams(
            collective_id=0, has_side_effects=True, vmem_limit_bytes=44 * 1024 * 1024
        ),
        name="join",
    )(positions.reshape(1, n_seq * rows), gate_logits, features, proj_weight)

    window = plan.window * 8
    block = 128 if rows_here % 128 == 0 else rows_here
    return pl.pallas_call(
        place_kernel,
        grid=(rows_here // block,),
        out_shape=jax.ShapeDtypeStruct(text.shape, text.dtype),
        in_specs=[
            pl.BlockSpec((1, window), lambda i: (0, 0)),
            pl.BlockSpec((plan.window, 8, depth), lambda i: (0, 0, 0)),
            pl.BlockSpec((block, depth), lambda i: (i, 0)),
        ],
        out_specs=pl.BlockSpec((block, depth), lambda i: (i, 0)),
        compiler_params=pltpu.CompilerParams(vmem_limit_bytes=24 * 1024 * 1024),
        name="place",
    )(local_rows, summed, text)


def solution(mesh):
    return jax.shard_map(
        shards,
        mesh=mesh,
        in_specs=(P("seq", "tp"), P(), P("tp", None), P(), P(("seq", "tp"), None)),
        out_specs=P(("seq", "tp"), None),
        check_vma=False,
    )
```
